32 devices in a mesh: dp: 2 (over y), gx: 4 (over z), gy: 4 (over x, core).
Axes of the slice: x: 2, y: 2, z: 4, core: 2. Of those that a mesh axis runs over, the one named last changes fastest.
Arguments:
- block_input: bfloat16 [3, 2, 2048, 1280], P(None, 'dp', ('gx', 'gy')), may hold values from -6 to 6
- picture: int32 [3, 2, 2048], P(None, 'dp'), may hold values from 0 to 24, as said below
- position: int32 [2, 3, 2, 2048], P(None, None, 'dp'), may hold values from 0 to 31, as said below
- patch_mask: int32 [3, 2, 2048], P(None, 'dp'), may hold values from 0 to 1, as said below
- gain_attn: float32 [1280], replicated, may hold values from 0.5 to 1.5
- shift_attn: float32 [1280], replicated, may hold values from -3 to 3
- w_query: bfloat16 [1280, 1280], P(('dp', 'gx'), 'gy'), may hold values from -0.15625 to 0.15625
- b_query: float32 [1280], replicated, may hold values from -3 to 3
- w_key: bfloat16 [1280, 1280], P(('dp', 'gx'), 'gy'), may hold values from -0.15625 to 0.15625
- b_key: float32 [1280], replicated, may hold values from -3 to 3
- w_value: bfloat16 [1280, 1280], P(('dp', 'gx'), 'gy'), may hold values from -0.15625 to 0.15625
- b_value: float32 [1280], replicated, may hold values from -3 to 3
- w_out: bfloat16 [1280, 1280], P(('dp', 'gx'), 'gy'), may hold values from -1.25 to 1.25
- b_out: float32 [1280], replicated, may hold values from -3 to 3
- gain_mlp: float32 [1280], replicated, may hold values from 0.5 to 1.5
- shift_mlp: float32 [1280], replicated, may hold values from -3 to 3
- w_up: bfloat16 [1280, 5120], P(('dp', 'gx'), 'gy'), may hold values from -0.15625 to 0.15625
- b_up: float32 [5120], replicated, may hold values from -3 to 3
- w_down: bfloat16 [1280, 5120], P(('dp', 'gx'), 'gy'), may hold values from -0.15625 to 0.15625
- b_down: float32 [1280], replicated, may hold values from -3 to 3
- out_grad: bfloat16 [3, 2, 2048, 1280], P(None, 'dp', ('gx', 'gy')), may hold values from -6 to 6
Outputs:
- block_output: bfloat16 [3, 2, 2048, 1280], P(None, 'dp', ('gx', 'gy'))
- input_grad: float32 [3, 2, 2048, 1280], P(None, 'dp', ('gx', 'gy'))
- gain_attn_grad: float32 [1280], replicated
- shift_attn_grad: float32 [1280], replicated
- w_query_grad: float32 [1280, 1280], P(('dp', 'gx'), 'gy')
- b_query_grad: float32 [1280], replicated
- w_key_grad: float32 [1280, 1280], P(('dp', 'gx'), 'gy')
- b_key_grad: float32 [1280], replicated
- w_value_grad: float32 [1280, 1280], P(('dp', 'gx'), 'gy')
- b_value_grad: float32 [1280], replicated
- w_out_grad: float32 [1280, 1280], P(('dp', 'gx'), 'gy')
- b_out_grad: float32 [1280], replicated
- gain_mlp_grad: float32 [1280], replicated
- shift_mlp_grad: float32 [1280], replicated
- w_up_grad: float32 [1280, 5120], P(('dp', 'gx'), 'gy')
- b_up_grad: float32 [5120], replicated
- w_down_grad: float32 [1280, 5120], P(('dp', 'gx'), 'gy')
- b_down_grad: float32 [1280], replicated
The draws below stay inside these ranges and needn't reach their ends.
Inputs may be any that keep to these rules, and one draw needn't show every extreme that they name: Each row holds whole pictures one after another from slot 0, numbered 0, 1, 2, ... in that order; every picture has h by w patches, one of each row 32 by 32 and the others with sides from 10 to 31; the slots after the last picture, at least one a row, hold 24. position[0] and position[1] are the row and column of a patch within its picture, in row-major order; padding slots hold 0. `patch_mask`: 1 on the slots of pictures, 0 on the padding after them.
All inputs are finite; a program needn't handle non-finite values.
Results may differ from the reference program's by a relative error of at most 0.02.
Values may be sent and summed in bfloat16 or wider, within the bound.
No kernel may reach another device: no remote copies, remote signals or barrier semaphores. Data moves between devices by JAX's collectives and lax.ppermute only.
A program may use at most 144 MiB of HBM per device.

```python
import jax
import jax.numpy as jnp
from jax import lax

D = 1280
HEADS = 16
HEAD_DIM = 80
FF = 5120
SLOTS = 2048
SIDE = 32
MIN_SIDE = 10
CAND = 24
MICRO = 3
ROWS = 2


def layout(key):
    base = jax.random.fold_in(key, 17)
    first, second, third = jax.random.split(base, 3)
    heights = jax.random.randint(first, (MICRO, ROWS, CAND), MIN_SIDE, SIDE)
    widths = jax.random.randint(second, (MICRO, ROWS, CAND), MIN_SIDE, SIDE)
    chosen = jax.random.randint(third, (MICRO, ROWS, 1), 0, 2)
    order = jnp.arange(CAND)
    heights = jnp.where(order == chosen, SIDE, heights)
    widths = jnp.where(order == chosen, SIDE, widths)
    lengths = heights * widths
    ends = jnp.cumsum(lengths, axis=-1)
    starts = ends - lengths
    fits = ends < SLOTS
    places = jnp.arange(SLOTS)[:, None]
    inside = (places >= starts[:, :, None, :]) & (places < ends[:, :, None, :]) & fits[:, :, None, :]
    inside = inside.astype(jnp.int32)
    used = jnp.sum(inside, axis=-1)
    numbers = jnp.sum(inside * order, axis=-1) + (1 - used) * CAND
    offset = jnp.arange(SLOTS) - jnp.sum(inside * starts[:, :, None, :], axis=-1)
    stride = jnp.maximum(jnp.sum(inside * widths[:, :, None, :], axis=-1), 1)
    row_place = offset // stride * used
    col_place = offset % stride * used
    return (numbers, jnp.stack([row_place, col_place]), used)


def draw_picture(key, part):
    return layout(key)[0]


def draw_position(key, part):
    return layout(key)[1]


def draw_patch_mask(key, part):
    return layout(key)[2]


def block_scale(key, shape, cuts, least, top_value):
    loudness, own = 1.0, jax.random.fold_in(key, 6)
    for dim, shards_of in cuts:
        draws = jnp.exp(jax.random.uniform(jax.random.fold_in(own, dim), (shards_of,), jnp.float32, least / len(cuts), top_value / len(cuts)))
        loudness = loudness * jnp.repeat(draws, shape[dim] // shards_of).reshape([-1 if axis == dim else 1 for axis in range(len(shape))])
    return loudness


def centred(stream_key, dims, scale, reach, shards=(), kind=jnp.bfloat16):
    values = jax.random.normal(stream_key, dims, jnp.float32) * scale
    if len(shards) > 0:
        values = block_scale(stream_key, dims, shards, -0.22, 0.18) * values
    return jnp.clip(values, min=-reach, max=reach).astype(kind)


def setup_inputs(seed: int = 0) -> dict:
    key_of = jax.random.split(jax.random.key(seed), 22)
    block_input = centred(key_of[0], (MICRO, ROWS, SLOTS, D), 1.0, 6.0, ((1, 2), (2, 16)))
    picture = draw_picture(jax.random.fold_in(key_of[21], 71), 0)
    position = draw_position(jax.random.fold_in(key_of[21], 71), 0)
    patch_mask = draw_patch_mask(jax.random.fold_in(key_of[21], 71), 0)
    gain_attn = jnp.clip(1.0 + 0.1 * jax.random.normal(key_of[4], (D,), jnp.float32), 0.5, 1.5)
    shift_attn = centred(key_of[5], (D,), 0.5, 3.0, (), jnp.float32)
    w_query = centred(key_of[6], (D, D), D ** -0.5, 0.15625, ((0, 8), (1, 4)))
    b_query = centred(key_of[7], (D,), 0.5, 3.0, (), jnp.float32)
    w_key = centred(key_of[8], (D, D), D ** -0.5, 0.15625, ((0, 8), (1, 4)))
    b_key = centred(key_of[9], (D,), 0.5, 3.0, (), jnp.float32)
    w_value = centred(key_of[10], (D, D), D ** -0.5, 0.15625, ((0, 8), (1, 4)))
    b_value = centred(key_of[11], (D,), 0.5, 3.0, (), jnp.float32)
    w_out = centred(key_of[12], (D, D), (HEAD_DIM // 4) ** -0.5, 1.25, ((0, 8), (1, 4)))
    b_out = centred(key_of[13], (D,), 0.5, 3.0, (), jnp.float32)
    gain_mlp = jnp.clip(1.0 + 0.1 * jax.random.normal(key_of[14], (D,), jnp.float32), 0.5, 1.5)
    shift_mlp = centred(key_of[15], (D,), 0.5, 3.0, (), jnp.float32)
    w_up = centred(key_of[16], (D, FF), D ** -0.5, 0.15625, ((0, 8), (1, 4)))
    b_up = centred(key_of[17], (FF,), 0.5, 3.0, (), jnp.float32)
    w_down = centred(key_of[18], (D, FF), (FF // 4) ** -0.5, 0.15625, ((0, 8), (1, 4)))
    b_down = centred(key_of[19], (D,), 0.5, 3.0, (), jnp.float32)
    out_grad = centred(key_of[20], (MICRO, ROWS, SLOTS, D), 1.0, 6.0, ((1, 2), (2, 16)))
    return dict(block_input=block_input, picture=picture, position=position, patch_mask=patch_mask, gain_attn=gain_attn, shift_attn=shift_attn, w_query=w_query, b_query=b_query, w_key=w_key, b_key=b_key, w_value=w_value, b_value=b_value, w_out=w_out, b_out=b_out, gain_mlp=gain_mlp, shift_mlp=shift_mlp, w_up=w_up, b_up=b_up, w_down=w_down, b_down=b_down, out_grad=out_grad)


@jax.custom_vjp
def low(v):
    return lax.optimization_barrier(v.astype(jnp.bfloat16)).astype(jnp.float32)

@jax.custom_vjp
def low_back(v):
    return v

def low_keep(v):
    return (low(v), None)

def low_pass(kept, grad):
    return (grad,)

def back_keep(v):
    return (v, None)

def back_low(kept, grad):
    return (low(grad),)
low.defvjp(low_keep, low_pass)
low_back.defvjp(back_keep, back_low)
HIGHEST = lax.Precision.HIGHEST

def matmul(left, right):
    return jnp.dot(left, right, precision=HIGHEST, preferred_element_type=jnp.float32)

def layer_norm(values, norm_gain, norm_shift):
    center = values - lax.optimization_barrier(jnp.mean(values, axis=-1, keepdims=True))
    spread = lax.optimization_barrier(jnp.mean(center * center, axis=-1, keepdims=True))
    return center * lax.rsqrt(spread + 1e-06) * norm_gain + norm_shift

def rotary_tables(position_row):
    quarter = HEAD_DIM // 4
    inverse = 10000.0 ** (-jnp.arange(quarter, dtype=jnp.float32) / quarter)
    along_rows = position_row[0].astype(jnp.float32)[:, None] * inverse
    along_cols = position_row[1].astype(jnp.float32)[:, None] * inverse
    angles = jnp.concatenate([along_rows, along_cols, along_rows, along_cols], axis=-1)[:, None, :]
    return (jnp.cos(angles), jnp.sin(angles))

def rotate(values, cos_table, sin_table):
    halfway = HEAD_DIM // 2
    turned = jnp.concatenate([-values[..., halfway:], values[..., :halfway]], axis=-1)
    return values * cos_table + turned * sin_table

def row_forward(params, inputs, picture_row, position_row, mask_row):
    gain_attn, shift_attn, w_query, b_query, w_key, b_key, w_value, b_value, w_out, b_out, gain_mlp, shift_mlp, w_up, b_up, w_down, b_down = params
    slot_count = inputs.shape[0]
    cos_table, sin_table = rotary_tables(position_row)
    normed = low(layer_norm(inputs, gain_attn, shift_attn))
    queries = low_back(matmul(normed, w_query) + b_query).reshape(slot_count, HEADS, HEAD_DIM)
    queries = low(rotate(queries, cos_table, sin_table))
    keys = low_back(matmul(normed, w_key) + b_key).reshape(slot_count, HEADS, HEAD_DIM)
    keys = low(rotate(keys, cos_table, sin_table))
    values = low(low_back(matmul(normed, w_value) + b_value)).reshape(slot_count, HEADS, HEAD_DIM)
    scores = jnp.einsum('qhd,khd->hqk', queries, keys, precision=HIGHEST) * HEAD_DIM ** (-0.5)
    scores = low_back(scores)
    places = jnp.arange(slot_count)
    visible = (picture_row[:, None] == picture_row[None, :]) & (mask_row[None, :] == 1) | (places[:, None] == places[None, :])
    scores = jnp.where(visible[None], scores, -1e+30)
    highest = lax.optimization_barrier(jnp.max(scores, axis=-1, keepdims=True))
    raised = jnp.exp(scores - highest)
    attend = low(raised / lax.optimization_barrier(jnp.sum(raised, axis=-1, keepdims=True)))
    mixture = jnp.einsum('hqk,khd->qhd', attend, values, precision=HIGHEST).reshape(slot_count, HEADS * HEAD_DIM)
    mixture = low(low_back(mixture))
    branch = low_back(matmul(mixture, w_out.T) + b_out)
    middle = inputs + branch
    normed_two = low(layer_norm(middle, gain_mlp, shift_mlp))
    hidden = low_back(matmul(normed_two, w_up) + b_up)
    active = low(hidden * jax.nn.sigmoid(1.702 * hidden))
    result = low_back(matmul(active, w_down.T) + b_down)
    return middle + result

def reference(block_input, picture, position, patch_mask, gain_attn, shift_attn, w_query, b_query, w_key, b_key, w_value, b_value, w_out, b_out, gain_mlp, shift_mlp, w_up, b_up, w_down, b_down, out_grad):
    params = (gain_attn, shift_attn, w_query.astype(jnp.float32), b_query, w_key.astype(jnp.float32), b_key, w_value.astype(jnp.float32), b_value, w_out.astype(jnp.float32), b_out, gain_mlp, shift_mlp, w_up.astype(jnp.float32), b_up, w_down.astype(jnp.float32), b_down)
    row_total = MICRO * ROWS
    inputs_all = block_input.reshape(row_total, SLOTS, D)
    cotangents = out_grad.reshape(row_total, SLOTS, D)
    pictures_all = picture.reshape(row_total, SLOTS)
    masks_all = patch_mask.reshape(row_total, SLOTS)
    positions_all = jnp.transpose(position.reshape(2, row_total, SLOTS), (1, 0, 2))
    empty_sums = jax.tree.map(jnp.zeros_like, params)

    def one_row(totals, sample):
        inputs, picture_row, position_row, mask_row, cotangent = sample

        def forward(weights, activations):
            return row_forward(weights, activations, picture_row, position_row, mask_row)
        result, pullback = jax.vjp(forward, params, inputs.astype(jnp.float32))
        weight_grads, input_grad = pullback(cotangent.astype(jnp.float32))
        totals = jax.tree.map(jnp.add, totals, weight_grads)
        return (totals, (result.astype(jnp.bfloat16), input_grad))
    totals, (outputs, input_grads) = lax.scan(one_row, empty_sums, (inputs_all, pictures_all, positions_all, masks_all, cotangents))
    block_output = outputs.reshape(MICRO, ROWS, SLOTS, D)
    input_grad = input_grads.reshape(MICRO, ROWS, SLOTS, D)
    return (block_output, input_grad, totals[0], totals[1], totals[2], totals[3], totals[4], totals[5], totals[6], totals[7], totals[8], totals[9], totals[10], totals[11], totals[12], totals[13], totals[14], totals[15])
```

```python
import functools

import jax
import jax.numpy as jnp
from jax import lax
from jax.experimental import pallas as pl
from jax.experimental.pallas import tpu as pltpu
from jax.sharding import PartitionSpec as P

HEAD_DIM = 80
HALF = HEAD_DIM // 2
PACK = 256
EPSILON = 1e-06
MAP = (0, 2, 1, 3)
BLK = 256
LOG2E = 1.4426950408889634
SCALE = HEAD_DIM ** (-0.5)
F32 = jnp.float32
BF16 = jnp.bfloat16
NT = (((1,), (1,)), ((), ()))


def dot(a, b):
    return jnp.dot(a, b, preferred_element_type=F32)


def dot_nt(a, b):
    return lax.dot_general(a, b, NT, preferred_element_type=F32)


def turn(v):
    return jnp.transpose(v.astype(F32))


VM = pl.BlockSpec(memory_space=pltpu.VMEM)
SM = pl.BlockSpec(memory_space=pltpu.SMEM)


def call(body, specs, outs, scratch, flops, nbytes, name, trans=0):
    return pl.pallas_call(
        body,
        in_specs=specs,
        out_specs=[VM] * len(outs),
        out_shape=[jax.ShapeDtypeStruct(s, d) for s, d in outs],
        scratch_shapes=[pltpu.VMEM(s, d) for s, d in scratch],
        cost_estimate=pl.CostEstimate(flops=flops, bytes_accessed=nbytes, transcendentals=trans),
        name=name,
    )


def head_of(p, dup):
    return p if dup == 1 else lax.div(p, dup)


def place_rows(s_ref, pieces, out, rows):
    for p in range(4):
        c = lax.bitwise_xor(s_ref[1], MAP[p])
        out[pl.ds(pl.multiple_of(c * rows, rows), rows), :] = pieces[p // 2][
            (p % 2) * rows : (p % 2 + 1) * rows, :
        ]


def split_rows(s_ref, src, keep, send, rows):
    for p in range(4):
        c = lax.bitwise_xor(s_ref[1], MAP[p])
        dst = (keep, send)[p // 2]
        dst[(p % 2) * rows : (p % 2 + 1) * rows, :] = src[
            pl.ds(pl.multiple_of(c * rows, rows), rows), :
        ]


def qkv_body(gx, dup, rows, s_ref, xa, xb, w, b, cos, sin, *rest):
    outs, xn = rest[:gx], rest[gx]
    place_rows(s_ref, (xa, xb), xn, rows)
    for r in range(gx):
        hh = head_of(lax.rem(s_ref[0] + r, gx), dup)
        cols = pl.ds(pl.multiple_of(hh * PACK, PACK), PACK)
        t = turn(dot(xn[...], w[:, cols]) + b[:, cols])
        c, s = cos[...], sin[...]
        for k in (0, 1):
            lo = t[k * HEAD_DIM : k * HEAD_DIM + HALF]
            hi = t[k * HEAD_DIM + HALF : (k + 1) * HEAD_DIM]
            both = jnp.concatenate([lo * c - hi * s, hi * c + lo * s], axis=0)
            outs[r][k * HEAD_DIM : (k + 1) * HEAD_DIM, :] = both.astype(BF16)
        outs[r][2 * HEAD_DIM : 3 * HEAD_DIM, :] = t[2 * HEAD_DIM : 3 * HEAD_DIM].astype(BF16)


def attend_body(gx, slots, s_ref, lim_ref, *rest):
    blocks = rest[:gx]
    idr, idc = rest[gx : gx + 2]
    outs = rest[gx + 2 : 2 * gx + 2]
    full, lse, mix, keys = rest[2 * gx + 2 :]
    qr = slots // gx
    nb = slots // BLK
    for r in range(gx):
        p = lax.rem(s_ref[0] + (gx - r), gx)
        full[:, pl.ds(pl.multiple_of(p * qr, qr), qr)] = blocks[r][...]
    for c in range(nb):
        keys[c * BLK : (c + 1) * BLK, :] = turn(
            full[HEAD_DIM : 2 * HEAD_DIM, c * BLK : (c + 1) * BLK]
        ).astype(BF16)

    def one(qb, carry):
        at = pl.ds(pl.multiple_of(qb * BLK, BLK), BLK)
        q = full[0:HEAD_DIM, at]
        qid = idr[:, at]

        def inner(kb, state):
            high, total, acc = state
            kat = pl.ds(pl.multiple_of(kb * BLK, BLK), BLK)
            s = dot(keys[kat, :], q)
            kid = idc[kat, :]
            kid = jnp.concatenate([kid] * (BLK // 128), axis=1)
            s = jnp.where(kid == qid, s * (SCALE * LOG2E), -1e30)
            top = jnp.maximum(high, jnp.max(s, axis=0, keepdims=True))
            e = jnp.exp2(s - top)
            fade = jnp.exp2(high - top)
            total = fade * total + jnp.sum(e, axis=0, keepdims=True)
            acc = fade * acc + dot(full[2 * HEAD_DIM : 3 * HEAD_DIM, kat], e.astype(BF16))
            return top, total, acc

        high, total, acc = lax.fori_loop(
            lim_ref[0, qb],
            lim_ref[1, qb] + 1,
            inner,
            (
                jnp.full((1, BLK), -1e30, F32),
                jnp.zeros((1, BLK), F32),
                jnp.zeros((HEAD_DIM, BLK), F32),
            ),
        )
        mix[:, at] = (acc / total).astype(BF16)
        lse[:, at] = high + jnp.log2(total)
        return carry

    lax.fori_loop(0, nb, one, 0)
    for r in range(gx):
        p = lax.rem(s_ref[0] + r, gx)
        outs[r][...] = mix[:, pl.ds(pl.multiple_of(p * qr, qr), qr)]


def project_body(gx, dup, rows, s_ref, *rest):
    blocks, wo = rest[:gx], rest[gx]
    mix, keep, send, flat, full = rest[gx + 1 :]
    for r in range(gx):
        hh = head_of(lax.rem(s_ref[0] + (gx - r), gx), dup)
        flat[pl.ds(pl.multiple_of(hh * HEAD_DIM, 16), HEAD_DIM), :] = blocks[r][...]
    mix[...] = turn(flat[...]).astype(BF16)
    full[...] = dot_nt(mix[...], wo[...]).astype(BF16)
    split_rows(s_ref, full, keep, send, rows)


def mlp_body(xa, xb, ca, cb, up, down, bias, act, hg, ra, rb, na, nb_, total):
    width = up.shape[1]
    depth = up.shape[0]
    n = xa.shape[0]
    total[...] = jnp.zeros_like(total)
    for h, (x, c, res, ng) in enumerate(((xb, cb, rb, nb_), (xa, ca, ra, na))):
        base = (1 - h) * n

        def first(t, carry):
            at = pl.ds(pl.multiple_of(t * 256, 256), 256)
            hidden = dot(x[...], up[:, at]) + bias[:, at]
            s = 1.0 / (1.0 + jnp.exp2(hidden * (-1.702 * LOG2E)))
            act[base : base + n, at] = (hidden * s).astype(BF16)
            g = dot(c[...], down[:, at]) * (s + 1.702 * hidden * s * (1.0 - s))
            g = g.astype(BF16)
            hg[base : base + n, at] = g
            total[:, at] = total[:, at] + jnp.sum(g.astype(F32), axis=0, keepdims=True)
            return carry

        lax.fori_loop(0, width // 256, first, 0)

        def second(t, carry):
            at = pl.ds(pl.multiple_of(t * 256, 256), 256)
            res[:, at] = dot_nt(act[base : base + n, :], down[at, :]).astype(BF16)
            ng[:, at] = dot_nt(hg[base : base + n, :], up[at, :]).astype(BF16)
            return carry

        lax.fori_loop(0, depth // 256, second, 0)


def mix_grad_body(gx, dup, rows, s_ref, ba, bb, wo, *rest):
    outs, brn, flat = rest[:gx], rest[gx], rest[gx + 1]
    place_rows(s_ref, (ba, bb), brn, rows)
    flat[...] = turn(dot(brn[...], wo[...])).astype(BF16)
    for r in range(gx):
        hh = head_of(lax.rem(s_ref[0] + r, gx), dup)
        outs[r][...] = flat[pl.ds(pl.multiple_of(hh * HEAD_DIM, 16), HEAD_DIM), :]


def attend_back_body(gx, slots, s_ref, lim_ref, *rest):
    full, lse, idr, idc, cos, sin = rest[:6]
    blocks = rest[6 : 6 + gx]
    outs = rest[6 + gx : 6 + 2 * gx]
    gt, kn, vn, qn, gn, es, gs, dk, dv, done = rest[6 + 2 * gx :]
    qr = slots // gx
    nb = slots // BLK
    for r in range(gx):
        p = lax.rem(s_ref[0] + (gx - r), gx)
        gt[:, pl.ds(pl.multiple_of(p * qr, qr), qr)] = blocks[r][...]
    for c in range(nb):
        at = slice(c * BLK, (c + 1) * BLK)
        qn[at, :] = turn(full[0:HEAD_DIM, at]).astype(BF16)
        kn[at, :] = turn(full[HEAD_DIM : 2 * HEAD_DIM, at]).astype(BF16)
        vn[at, :] = turn(full[2 * HEAD_DIM : 3 * HEAD_DIM, at]).astype(BF16)
        gn[at, :] = turn(gt[:, at]).astype(BF16)
    dk[...] = jnp.zeros_like(dk)
    dv[...] = jnp.zeros_like(dv)

    def one(qb, carry):
        at = pl.ds(pl.multiple_of(qb * BLK, BLK), BLK)
        first, past = lim_ref[0, qb], lim_ref[1, qb] + 1

        def scores(kb, delta):
            kat = pl.ds(pl.multiple_of(kb * BLK, BLK), BLK)
            s = dot(kn[kat, :], full[0:HEAD_DIM, at])
            kid = idc[kat, :]
            kid = jnp.concatenate([kid] * (BLK // 128), axis=1)
            e = jnp.where(
                kid == idr[:, at], jnp.exp2(s * (SCALE * LOG2E) - lse[:, at]), 0.0
            )
            g = dot(vn[kat, :], gt[:, at])
            es[kat, :] = e
            gs[kat, :] = g
            return delta + jnp.sum(e * g, axis=0, keepdims=True)

        delta = lax.fori_loop(first, past, scores, jnp.zeros((1, BLK), F32))

        def grads(kb, dq):
            kat = pl.ds(pl.multiple_of(kb * BLK, BLK), BLK)
            e = es[kat, :]
            ds = (e * (gs[kat, :] - delta)).astype(BF16)
            dv[kat, :] += dot(e.astype(BF16), gn[at, :])
            dk[kat, :] += dot(ds, qn[at, :])
            return dq + dot(full[HEAD_DIM : 2 * HEAD_DIM, kat], ds)

        dq = lax.fori_loop(first, past, grads, jnp.zeros((HEAD_DIM, BLK), F32)) * SCALE
        c, s = cos[:, at], sin[:, at]
        lo, hi = dq[:HALF], dq[HALF:]
        done[0:HEAD_DIM, at] = jnp.concatenate(
            [lo * c + hi * s, hi * c - lo * s], axis=0
        ).astype(BF16)
        return carry

    lax.fori_loop(0, nb, one, 0)

    def finish(kb, carry):
        at = pl.ds(pl.multiple_of(kb * BLK, BLK), BLK)
        c, s = cos[:, at], sin[:, at]
        back = turn(dk[at, :]) * SCALE
        lo, hi = back[:HALF], back[HALF:]
        done[HEAD_DIM : 2 * HEAD_DIM, at] = jnp.concatenate(
            [lo * c + hi * s, hi * c - lo * s], axis=0
        ).astype(BF16)
        done[2 * HEAD_DIM : 3 * HEAD_DIM, at] = turn(dv[at, :]).astype(BF16)
        return carry

    lax.fori_loop(0, nb, finish, 0)
    for r in range(gx):
        p = lax.rem(s_ref[0] + r, gx)
        outs[r][...] = done[:, pl.ds(pl.multiple_of(p * qr, qr), qr)]


def qkv_back_body(gx, dup, rows, s_ref, *rest):
    blocks, w = rest[:gx], rest[gx]
    d, keep, send, total, full = rest[gx + 1 :]
    for r in range(gx):
        hh = head_of(lax.rem(s_ref[0] + (gx - r), gx), dup)
        t = blocks[r][...].astype(F32)
        t = jnp.concatenate([t, jnp.zeros((PACK - 3 * HEAD_DIM, t.shape[1]), F32)], axis=0)
        d[:, pl.ds(pl.multiple_of(hh * PACK, PACK), PACK)] = jnp.transpose(t).astype(BF16)
    total[...] = jnp.sum(d[...].astype(F32), axis=0, keepdims=True)

    def step(t, carry):
        at = pl.ds(pl.multiple_of(t * 256, 256), 256)
        full[:, at] = dot_nt(d[...], w[at, :]).astype(BF16)
        return carry

    lax.fori_loop(0, w.shape[0] // 256, step, 0)
    split_rows(s_ref, full, keep, send, rows)


def weight_grad_body(n, *rest):
    left, right, out = rest[:n], rest[n : 2 * n], rest[2 * n]

    def step(t, carry):
        at = pl.ds(pl.multiple_of(t * 256, 256), 256)
        acc = None
        for a, b in zip(left, right):
            part = lax.dot_general(
                a[:, at], b[...], (((0,), (0,)), ((), ())), preferred_element_type=F32
            )
            acc = part if acc is None else acc + part
        out[at, :] = acc.astype(BF16)
        return carry

    lax.fori_loop(0, out.shape[0] // 256, step, 0)


def weight_grad(left, right, name):
    d1, d2 = left[0].shape[1], right[0].shape[1]
    k = sum(a.shape[0] for a in left)
    n = len(left)
    return call(
        functools.partial(weight_grad_body, n),
        [VM] * (2 * n),
        [((d1, d2), BF16)],
        [],
        2 * k * d1 * d2,
        2 * (k * (d1 + d2) + d1 * d2),
        name,
    )(*left, *right)[0]


def layer_norm(values, norm_gain, norm_shift):
    center = values - jnp.mean(values, axis=-1, keepdims=True)
    factor = lax.rsqrt(jnp.mean(center * center, axis=-1, keepdims=True) + EPSILON)
    normal = center * factor
    return (normal * norm_gain + norm_shift, normal, factor)


def norm_back(upstream, normal, factor, norm_gain):
    shaped = upstream * norm_gain
    first_mean = jnp.mean(shaped, axis=-1, keepdims=True)
    second_mean = jnp.mean(shaped * normal, axis=-1, keepdims=True)
    return factor * (shaped - first_mean - normal * second_mean)


def per_device(
    block_input,
    picture,
    position,
    patch_mask,
    gain_attn,
    shift_attn,
    w_query,
    b_query,
    w_key,
    b_key,
    w_value,
    b_value,
    w_out,
    b_out,
    gain_mlp,
    shift_mlp,
    w_up,
    b_up,
    w_down,
    b_down,
    out_grad,
):
    gx = lax.axis_size("gx")
    column = lax.axis_index("gy")
    segment = lax.axis_index("gx")
    micros = block_input.shape[0]
    rows = block_input.shape[2]
    width = block_input.shape[3]
    slots = picture.shape[2]
    qr = 4 * rows
    head_cols = w_query.shape[1]
    hidden_cols = w_up.shape[1]
    heads = head_cols // HEAD_DIM
    dup = gx // heads
    assert lax.axis_size("gy") == 4 and dup * heads == gx and slots == qr * gx
    shard_rows = w_query.shape[0]
    head_start = column * head_cols
    up_start = column * hidden_cols
    where = jnp.stack([segment, column]).astype(jnp.int32)
    x_pairs = [(d, d ^ 2) for d in range(4)]
    core_pairs = [(d, d ^ 1) for d in range(4)]
    spins = [[(d, (d + r) % gx) for d in range(gx)] for r in range(gx)]
    over = ("dp", "gx")

    def pack(q, k, v):
        n = q.shape[0]
        parts = [t.reshape(n, heads, HEAD_DIM) for t in (q, k, v)]
        parts.append(jnp.zeros((n, heads, PACK - 3 * HEAD_DIM), q.dtype))
        return jnp.concatenate(parts, axis=2).reshape(n, heads * PACK)

    def unpack(t):
        n = t.shape[0]
        t = t.reshape(n, heads, PACK)
        return [
            t[:, :, k * HEAD_DIM : (k + 1) * HEAD_DIM].reshape(n, head_cols) for k in range(3)
        ]

    full_qkv = lax.all_gather(pack(w_query, w_key, w_value), over, axis=0, tiled=True)
    full_out = lax.all_gather(w_out, over, axis=0, tiled=True)
    full_up = lax.all_gather(w_up, over, axis=0, tiled=True)
    full_down = lax.all_gather(w_down, over, axis=0, tiled=True)
    biases = [
        lax.dynamic_slice_in_dim(b, head_start, head_cols)[None] for b in (b_query, b_key, b_value)
    ]
    qkv_bias = pack(*biases)
    up_bias = lax.dynamic_slice_in_dim(b_up, up_start, hidden_cols)[None]

    def spread(v):
        half = jnp.concatenate([v, lax.ppermute(v, "gy", x_pairs)], axis=0)
        return half, lax.ppermute(half, "gy", core_pairs)

    def collect(keep, send):
        both = keep.astype(F32) + lax.ppermute(send, "gy", core_pairs).astype(F32)
        return both[:rows] + lax.ppermute(both[rows:].astype(BF16), "gy", x_pairs).astype(F32)

    def swap(blocks):
        return [blocks[0]] + [lax.ppermute(blocks[r], "gx", spins[r]) for r in range(1, gx)]

    quarter = HEAD_DIM // 4
    inverse = 10000.0 ** (-jnp.arange(quarter, dtype=F32) / quarter)
    places = position[:, :, 0, :].astype(F32)
    angles = jnp.concatenate(
        [inverse[None, :, None] * places[0][:, None], inverse[None, :, None] * places[1][:, None]],
        axis=1,
    )
    cos_all, sin_all = jnp.cos(angles), jnp.sin(angles)
    cos_own = lax.dynamic_slice_in_dim(cos_all, segment * qr, qr, 2)
    sin_own = lax.dynamic_slice_in_dim(sin_all, segment * qr, qr, 2)

    pictures, masks = picture[:, 0], patch_mask[:, 0]
    marks = jnp.where(masks == 1, pictures, 1000 + jnp.arange(slots, dtype=jnp.int32)[None])
    id_row = marks[:, None, :]
    id_col = jnp.broadcast_to(marks[:, :, None], (micros, slots, 128))
    nb = slots // BLK
    own_block = jnp.arange(nb, dtype=jnp.int32)[None]
    first_id, last_id = pictures[:, ::BLK], pictures[:, BLK - 1 :: BLK]
    below = jnp.sum(
        (pictures[:, None, :] < first_id[:, :, None]).astype(jnp.int32), axis=-1
    )
    upto = jnp.sum(
        (pictures[:, None, :] <= last_id[:, :, None]).astype(jnp.int32), axis=-1
    )
    low = jnp.where(masks[:, ::BLK] == 1, below // BLK, own_block)
    top = jnp.where(masks[:, BLK - 1 :: BLK] == 1, (upto - 1) // BLK, own_block)
    limits = jnp.stack([low, top], axis=1)

    tri = 3 * HEAD_DIM
    qkv_call = call(
        functools.partial(qkv_body, gx, dup, rows),
        [SM] + [VM] * 6,
        [((tri, qr), BF16)] * gx + [((qr, width), BF16)],
        [],
        2 * qr * width * gx * PACK,
        2 * (2 * qr * width + width * heads * PACK + gx * tri * qr),
        "qkv",
    )
    work = slots * slots // 2
    attend_call = call(
        functools.partial(attend_body, gx, slots),
        [SM, SM] + [VM] * (gx + 2),
        [((HEAD_DIM, qr), BF16)] * gx
        + [((tri, slots), BF16), ((1, slots), F32)],
        [((HEAD_DIM, slots), BF16), ((slots, HEAD_DIM), BF16)],
        4 * work * PACK,
        2 * 10 * HEAD_DIM * slots,
        "attend",
        work,
    )
    project_call = call(
        functools.partial(project_body, gx, dup, rows),
        [SM] + [VM] * (gx + 1),
        [((qr, head_cols), BF16), ((2 * rows, width), BF16), ((2 * rows, width), BF16)],
        [((head_cols, qr), BF16), ((qr, width), BF16)],
        2 * qr * width * head_cols,
        2 * (2 * qr * head_cols + width * head_cols + qr * width),
        "project",
    )
    half_rows = ((2 * rows, width), BF16)
    mlp_call = call(
        mlp_body,
        [VM] * 7,
        [((qr, hidden_cols), BF16)] * 2 + [half_rows] * 4 + [((1, hidden_cols), F32)],
        [],
        8 * qr * width * hidden_cols,
        2 * (4 * qr * width + 2 * width * hidden_cols + 2 * qr * hidden_cols),
        "mlp",
    )
    mix_grad_call = call(
        functools.partial(mix_grad_body, gx, dup, rows),
        [SM] + [VM] * 3,
        [((HEAD_DIM, qr), BF16)] * gx + [((qr, width), BF16)],
        [((head_cols, qr), BF16)],
        2 * qr * width * head_cols,
        2 * (2 * qr * width + width * head_cols + qr * head_cols),
        "mix_grad",
    )
    attend_back_call = call(
        functools.partial(attend_back_body, gx, slots),
        [SM, SM] + [VM] * (6 + gx),
        [((tri, qr), BF16)] * gx,
        [((HEAD_DIM, slots), BF16)]
        + [((slots, HEAD_DIM), BF16)] * 4
        + [((slots, BLK), F32)] * 2
        + [((slots, HEAD_DIM), F32)] * 2
        + [((tri, slots), BF16)],
        10 * work * PACK,
        2 * 10 * HEAD_DIM * slots,
        "attend_back",
        work,
    )
    qkv_back_call = call(
        functools.partial(qkv_back_body, gx, dup, rows),
        [SM] + [VM] * (gx + 1),
        [((qr, heads * PACK), BF16), half_rows, half_rows, ((1, heads * PACK), F32)],
        [((qr, width), BF16)],
        2 * qr * width * heads * PACK,
        2 * (2 * qr * heads * PACK + width * heads * PACK + qr * width),
        "qkv_back",
    )

    inputs = block_input[:, 0].astype(F32)
    normed = layer_norm(inputs, gain_attn, shift_attn)[0].astype(BF16)
    cots = out_grad[:, 0]
    normed_x = lax.ppermute(normed, "gy", x_pairs)
    cots_x = lax.ppermute(cots, "gy", x_pairs)
    saved = []
    for m in range(micros):
        na = jnp.concatenate([normed[m], normed_x[m]], axis=0)
        nb_half = lax.ppermute(na, "gy", core_pairs)
        *sent, rows_in = qkv_call(
            where, na, nb_half, full_qkv, qkv_bias, cos_own[m], sin_own[m]
        )
        *mixed, qkv_full, log_total = attend_call(
            where, limits[m], *swap(sent), id_row[m], id_col[m]
        )
        saved.append((rows_in, qkv_full, log_total, swap(mixed)))

    vec_gain_mlp = vec_shift_mlp = vec_up = vec_out = 0.0
    second = []
    outputs = []
    for m in range(micros):
        mix, keep, send = project_call(where, *saved[m][3], full_out)
        middle = inputs[m] + collect(keep, send) + b_out
        normed_two, normal_two, factor_two = layer_norm(middle, gain_mlp, shift_mlp)
        xa, xb = spread(normed_two.astype(BF16))
        ca = jnp.concatenate([cots[m], cots_x[m]], axis=0)
        cb = lax.ppermute(ca, "gy", core_pairs)
        act, hg, ra, rb, na, nb_half, up_part = mlp_call(
            xa, xb, ca, cb, full_up, full_down, up_bias
        )
        vec_up = vec_up + up_part[0]
        two_grad = collect(na, nb_half)
        result = collect(ra, rb)
        outputs.append((middle + result + b_down).astype(BF16))
        vec_gain_mlp = vec_gain_mlp + jnp.sum(two_grad * normal_two, axis=0)
        vec_shift_mlp = vec_shift_mlp + jnp.sum(two_grad, axis=0)
        middle_grad = cots[m].astype(F32) + norm_back(two_grad, normal_two, factor_two, gain_mlp)
        branch_grad = middle_grad.astype(BF16)
        vec_out = vec_out + jnp.sum(branch_grad.astype(F32), axis=0)
        second.append((mix, xa, xb, ca, cb, act, hg, middle_grad, branch_grad))

    vec_gain_attn = vec_shift_attn = vec_qkv = 0.0
    input_grads = []
    last = []
    for m in range(micros):
        middle_grad, branch_grad = second[m][7:]
        rows_in, qkv_full, log_total, _ = saved[m]
        ba, bb = spread(branch_grad)
        *sent, branch_rows = mix_grad_call(where, ba, bb, full_out)
        got = attend_back_call(
            where,
            limits[m],
            qkv_full,
            log_total,
            id_row[m],
            id_col[m],
            cos_all[m],
            sin_all[m],
            *swap(sent),
        )
        d, keep, send, part = qkv_back_call(where, *swap(got), full_qkv)
        vec_qkv = vec_qkv + part
        one_grad = collect(keep, send)
        _, normal_one, factor_one = layer_norm(inputs[m], gain_attn, shift_attn)
        vec_gain_attn = vec_gain_attn + jnp.sum(one_grad * normal_one, axis=0)
        vec_shift_attn = vec_shift_attn + jnp.sum(one_grad, axis=0)
        input_grads.append(middle_grad + norm_back(one_grad, normal_one, factor_one, gain_attn))
        last.append((rows_in, d, branch_rows))

    def reduce(full):
        return lax.psum_scatter(full, over, scatter_dimension=0, tiled=True).astype(F32)

    grad_up = reduce(
        weight_grad(
            [t for s in second for t in s[1:3]],
            [s[6][h * 2 * rows : (h + 1) * 2 * rows] for s in second for h in (0, 1)],
            "grad_up",
        )
    )
    grad_down = reduce(
        weight_grad(
            [t for s in second for t in s[3:5]],
            [s[5][h * 2 * rows : (h + 1) * 2 * rows] for s in second for h in (0, 1)],
            "grad_down",
        )
    )
    grad_out = reduce(weight_grad([t[2] for t in last], [s[0] for s in second], "grad_out"))
    grad_qkv = reduce(weight_grad([t[0] for t in last], [t[1] for t in last], "grad_qkv"))
    grad_query, grad_key, grad_value = unpack(grad_qkv)

    def whole(part, start, total):
        return lax.dynamic_update_slice_in_dim(jnp.zeros((total,), F32), part, start, 0)

    vec_q, vec_k, vec_v = [whole(t[0], head_start, b_query.shape[0]) for t in unpack(vec_qkv)]
    vectors = lax.psum(
        (
            vec_gain_attn,
            vec_shift_attn,
            vec_q,
            vec_k,
            vec_v,
            vec_out,
            vec_gain_mlp,
            vec_shift_mlp,
            whole(vec_up, up_start, b_up.shape[0]),
            jnp.sum(cots.astype(F32), axis=(0, 1)),
        ),
        ("dp", "gx", "gy"),
    )
    return (
        jnp.stack(outputs)[:, None],
        jnp.stack(input_grads)[:, None],
        vectors[0],
        vectors[1],
        grad_query,
        vectors[2],
        grad_key,
        vectors[3],
        grad_value,
        vectors[4],
        grad_out,
        vectors[5],
        vectors[6],
        vectors[7],
        grad_up,
        vectors[8],
        grad_down,
        vectors[9],
    )


def solution(mesh):
    acts = P(None, "dp", ("gx", "gy"), None)
    ids = P(None, "dp", None)
    weight = P(("dp", "gx"), "gy")
    placed = (acts, ids, P(None, None, "dp", None), ids, P(), P())
    placed += (weight, P()) * 4 + (P(), P()) + (weight, P()) * 2 + (acts,)
    outs = (acts, acts, P(), P()) + (weight, P()) * 4 + (P(), P()) + (weight, P()) * 2
    return jax.shard_map(
        per_device, mesh=mesh, in_specs=placed, out_specs=outs, check_vma=False
    )
```

```python
import functools

import jax
import jax.numpy as jnp
from jax import lax
from jax.experimental import pallas as pl
from jax.experimental.pallas import tpu as pltpu
from jax.sharding import PartitionSpec as P

HEAD_DIM = 80
HALF = HEAD_DIM // 2
PACK = 256
EPSILON = 1e-06
MAP = (0, 2, 1, 3)
BLK = 256
SPARE = 4 << 20
COST = dict(
    join_qkv=1.2,
    join_rest=1.1,
    qkv=2.4,
    attend=11.5,
    project=2.0,
    mlp=12.1,
    mix_grad=1.6,
    attend_back=14.6,
    qkv_back=4.5,
    grad_up=8.1,
    grad_down=8.1,
    grad_out=3.8,
    grad_qkv=5.8,
    join_out=0.5,
)
LOG2E = 1.4426950408889634
SCALE = HEAD_DIM ** (-0.5)
F32 = jnp.float32
BF16 = jnp.bfloat16
NT = (((1,), (1,)), ((), ()))


def dot(a, b):
    return jnp.dot(a, b, preferred_element_type=F32)


def dot_nt(a, b):
    return lax.dot_general(a, b, NT, preferred_element_type=F32)


def turn(v):
    return jnp.transpose(v.astype(F32))


VM = pl.BlockSpec(memory_space=pltpu.VMEM)
SM = pl.BlockSpec(memory_space=pltpu.SMEM)


def room(shape, dtype):
    size = jnp.dtype(dtype).itemsize
    *lead, r, c = (1, 1) + tuple(shape)
    tile = 32 // size
    total = -(-r // tile) * tile * -(-c // 128) * 128 * size
    for n in lead:
        total *= n
    return total


def call(body, specs, outs, scratch, flops, nbytes, name, trans=0):
    def run(*args):
        held = sum(room(a.shape, a.dtype) for a, spec in zip(args, specs) if spec is VM)
        held += sum(room(*t) for t in outs) + sum(room(*t) for t in scratch)
        return pl.pallas_call(
            body,
            in_specs=specs,
            out_specs=[VM] * len(outs),
            out_shape=[jax.ShapeDtypeStruct(s, d) for s, d in outs],
            scratch_shapes=[pltpu.VMEM(s, d) for s, d in scratch],
            cost_estimate=pl.CostEstimate(
                flops=int(1.15e9 * COST[name]), bytes_accessed=0, transcendentals=0
            ),
            compiler_params=pltpu.CompilerParams(vmem_limit_bytes=held + SPARE),
            name=name,
        )(*args)

    return run


def head_of(p, dup):
    return p if dup == 1 else lax.div(p, dup)


def place_rows(s_ref, pieces, out, rows):
    for p in range(4):
        c = lax.bitwise_xor(s_ref[1], MAP[p])
        out[pl.ds(pl.multiple_of(c * rows, rows), rows), :] = pieces[p // 2][
            (p % 2) * rows : (p % 2 + 1) * rows, :
        ]


def split_rows(s_ref, src, keep, send, rows):
    for p in range(4):
        c = lax.bitwise_xor(s_ref[1], MAP[p])
        dst = (keep, send)[p // 2]
        dst[(p % 2) * rows : (p % 2 + 1) * rows, :] = src[
            pl.ds(pl.multiple_of(c * rows, rows), rows), :
        ]


def qkv_body(gx, dup, rows, s_ref, xa, xb, w, b, cos, sin, *rest):
    outs, xn = rest[:gx], rest[gx]
    place_rows(s_ref, (xa, xb), xn, rows)
    for r in range(gx):
        hh = head_of(lax.rem(s_ref[0] + r, gx), dup)
        cols = pl.ds(pl.multiple_of(hh * PACK, PACK), PACK)
        t = turn(dot(xn[...], w[:, cols]) + b[:, cols])
        c, s = cos[...], sin[...]
        for k in (0, 1):
            lo = t[k * HEAD_DIM : k * HEAD_DIM + HALF]
            hi = t[k * HEAD_DIM + HALF : (k + 1) * HEAD_DIM]
            both = jnp.concatenate([lo * c - hi * s, hi * c + lo * s], axis=0)
            outs[r][k * HEAD_DIM : (k + 1) * HEAD_DIM, :] = both.astype(BF16)
        outs[r][2 * HEAD_DIM : 3 * HEAD_DIM, :] = t[2 * HEAD_DIM : 3 * HEAD_DIM].astype(BF16)


def attend_body(gx, slots, s_ref, lim_ref, *rest):
    blocks = rest[:gx]
    idr, idc = rest[gx : gx + 2]
    outs = rest[gx + 2 : 2 * gx + 2]
    full, lse, mix, keys = rest[2 * gx + 2 :]
    qr = slots // gx
    nb = slots // BLK
    for r in range(gx):
        p = lax.rem(s_ref[0] + (gx - r), gx)
        full[:, pl.ds(pl.multiple_of(p * qr, qr), qr)] = blocks[r][...]
    for c in range(nb):
        keys[c * BLK : (c + 1) * BLK, :] = turn(
            full[HEAD_DIM : 2 * HEAD_DIM, c * BLK : (c + 1) * BLK]
        ).astype(BF16)

    def one(qb, carry):
        at = pl.ds(pl.multiple_of(qb * BLK, BLK), BLK)
        q = full[0:HEAD_DIM, at]
        qid = idr[:, at]

        def inner(kb, state):
            high, total, acc = state
            kat = pl.ds(pl.multiple_of(kb * BLK, BLK), BLK)
            s = dot(keys[kat, :], q)
            kid = idc[kat, :]
            kid = jnp.concatenate([kid] * (BLK // 128), axis=1)
            s = jnp.where(kid == qid, s * (SCALE * LOG2E), -1e30)
            top = jnp.maximum(high, jnp.max(s, axis=0, keepdims=True))
            e = jnp.exp2(s - top)
            fade = jnp.exp2(high - top)
            total = fade * total + jnp.sum(e, axis=0, keepdims=True)
            acc = fade * acc + dot(full[2 * HEAD_DIM : 3 * HEAD_DIM, kat], e.astype(BF16))
            return top, total, acc

        high, total, acc = lax.fori_loop(
            lim_ref[0, qb],
            lim_ref[1, qb] + 1,
            inner,
            (
                jnp.full((1, BLK), -1e30, F32),
                jnp.zeros((1, BLK), F32),
                jnp.zeros((HEAD_DIM, BLK), F32),
            ),
        )
        mix[:, at] = (acc / total).astype(BF16)
        lse[:, at] = high + jnp.log2(total)
        return carry

    lax.fori_loop(0, nb, one, 0)
    for r in range(gx):
        p = lax.rem(s_ref[0] + r, gx)
        outs[r][...] = mix[:, pl.ds(pl.multiple_of(p * qr, qr), qr)]


def project_body(gx, dup, rows, s_ref, *rest):
    blocks, wo = rest[:gx], rest[gx]
    mix, keep, send, flat, full = rest[gx + 1 :]
    for r in range(gx):
        hh = head_of(lax.rem(s_ref[0] + (gx - r), gx), dup)
        flat[pl.ds(pl.multiple_of(hh * HEAD_DIM, 16), HEAD_DIM), :] = blocks[r][...]
    mix[...] = turn(flat[...]).astype(BF16)
    full[...] = dot_nt(mix[...], wo[...]).astype(BF16)
    split_rows(s_ref, full, keep, send, rows)


def mlp_body(s_ref, xa, xb, ca, cb, up, down, bias, act, hg, ra, rb, na, nb_, total):
    width = up.shape[1]
    depth = up.shape[0]
    n = xa.shape[0]
    total[...] = jnp.zeros_like(total)
    for h, (x, c, res, ng) in enumerate(((xb, cb, rb, nb_), (xa, ca, ra, na))):
        base = (1 - h) * n

        def first(t, carry):
            at = pl.ds(pl.multiple_of(t * 256, 256), 256)
            hidden = dot(x[...], up[:, at]) + bias[:, at]
            s = 1.0 / (1.0 + jnp.exp2(hidden * (-1.702 * LOG2E)))
            act[base : base + n, at] = (hidden * s).astype(BF16)
            g = dot(c[...], down[:, at]) * (s + 1.702 * hidden * s * (1.0 - s))
            g = g.astype(BF16)
            hg[base : base + n, at] = g
            total[:, at] = total[:, at] + jnp.sum(g.astype(F32), axis=0, keepdims=True)
            return carry

        lax.fori_loop(0, width // 256, first, 0)

        def second(t, carry):
            at = pl.ds(pl.multiple_of(t * 256, 256), 256)
            res[:, at] = dot_nt(act[base : base + n, :], down[at, :]).astype(BF16)
            ng[:, at] = dot_nt(hg[base : base + n, :], up[at, :]).astype(BF16)
            return carry

        lax.fori_loop(0, depth // 256, second, 0)


def mix_grad_body(gx, dup, rows, s_ref, ba, bb, wo, *rest):
    outs, brn, flat = rest[:gx], rest[gx], rest[gx + 1]
    place_rows(s_ref, (ba, bb), brn, rows)
    flat[...] = turn(dot(brn[...], wo[...])).astype(BF16)
    for r in range(gx):
        hh = head_of(lax.rem(s_ref[0] + r, gx), dup)
        outs[r][...] = flat[pl.ds(pl.multiple_of(hh * HEAD_DIM, 16), HEAD_DIM), :]


def attend_back_body(gx, slots, s_ref, lim_ref, *rest):
    full, lse, idr, idc, cos, sin = rest[:6]
    blocks = rest[6 : 6 + gx]
    outs = rest[6 + gx : 6 + 2 * gx]
    gt, kn, vn, qn, gn, es, gs, dk, dv, done = rest[6 + 2 * gx :]
    qr = slots // gx
    nb = slots // BLK
    for r in range(gx):
        p = lax.rem(s_ref[0] + (gx - r), gx)
        gt[:, pl.ds(pl.multiple_of(p * qr, qr), qr)] = blocks[r][...]
    for c in range(nb):
        at = slice(c * BLK, (c + 1) * BLK)
        qn[at, :] = turn(full[0:HEAD_DIM, at]).astype(BF16)
        kn[at, :] = turn(full[HEAD_DIM : 2 * HEAD_DIM, at]).astype(BF16)
        vn[at, :] = turn(full[2 * HEAD_DIM : 3 * HEAD_DIM, at]).astype(BF16)
        gn[at, :] = turn(gt[:, at]).astype(BF16)
    dk[...] = jnp.zeros_like(dk)
    dv[...] = jnp.zeros_like(dv)

    def one(qb, carry):
        at = pl.ds(pl.multiple_of(qb * BLK, BLK), BLK)
        first, past = lim_ref[0, qb], lim_ref[1, qb] + 1

        def scores(kb, delta):
            kat = pl.ds(pl.multiple_of(kb * BLK, BLK), BLK)
            s = dot(kn[kat, :], full[0:HEAD_DIM, at])
            kid = idc[kat, :]
            kid = jnp.concatenate([kid] * (BLK // 128), axis=1)
            e = jnp.where(
                kid == idr[:, at], jnp.exp2(s * (SCALE * LOG2E) - lse[:, at]), 0.0
            )
            g = dot(vn[kat, :], gt[:, at])
            es[kat, :] = e
            gs[kat, :] = g
            return delta + jnp.sum(e * g, axis=0, keepdims=True)

        delta = lax.fori_loop(first, past, scores, jnp.zeros((1, BLK), F32))

        def grads(kb, dq):
            kat = pl.ds(pl.multiple_of(kb * BLK, BLK), BLK)
            e = es[kat, :]
            ds = (e * (gs[kat, :] - delta)).astype(BF16)
            dv[kat, :] += dot(e.astype(BF16), gn[at, :])
            dk[kat, :] += dot(ds, qn[at, :])
            return dq + dot(full[HEAD_DIM : 2 * HEAD_DIM, kat], ds)

        dq = lax.fori_loop(first, past, grads, jnp.zeros((HEAD_DIM, BLK), F32)) * SCALE
        c, s = cos[:, at], sin[:, at]
        lo, hi = dq[:HALF], dq[HALF:]
        done[0:HEAD_DIM, at] = jnp.concatenate(
            [lo * c + hi * s, hi * c - lo * s], axis=0
        ).astype(BF16)
        return carry

    lax.fori_loop(0, nb, one, 0)

    def finish(kb, carry):
        at = pl.ds(pl.multiple_of(kb * BLK, BLK), BLK)
        c, s = cos[:, at], sin[:, at]
        back = turn(dk[at, :]) * SCALE
        lo, hi = back[:HALF], back[HALF:]
        done[HEAD_DIM : 2 * HEAD_DIM, at] = jnp.concatenate(
            [lo * c + hi * s, hi * c - lo * s], axis=0
        ).astype(BF16)
        done[2 * HEAD_DIM : 3 * HEAD_DIM, at] = turn(dv[at, :]).astype(BF16)
        return carry

    lax.fori_loop(0, nb, finish, 0)
    for r in range(gx):
        p = lax.rem(s_ref[0] + r, gx)
        outs[r][...] = done[:, pl.ds(pl.multiple_of(p * qr, qr), qr)]


def qkv_back_body(gx, dup, rows, s_ref, *rest):
    blocks, w = rest[:gx], rest[gx]
    d, keep, send, total, full = rest[gx + 1 :]
    for r in range(gx):
        hh = head_of(lax.rem(s_ref[0] + (gx - r), gx), dup)
        t = blocks[r][...].astype(F32)
        t = jnp.concatenate([t, jnp.zeros((PACK - 3 * HEAD_DIM, t.shape[1]), F32)], axis=0)
        d[:, pl.ds(pl.multiple_of(hh * PACK, PACK), PACK)] = jnp.transpose(t).astype(BF16)
    total[...] = jnp.sum(d[...].astype(F32), axis=0, keepdims=True)

    def step(t, carry):
        at = pl.ds(pl.multiple_of(t * 256, 256), 256)
        full[:, at] = dot_nt(d[...], w[at, :]).astype(BF16)
        return carry

    lax.fori_loop(0, w.shape[0] // 256, step, 0)
    split_rows(s_ref, full, keep, send, rows)


def weight_grad_body(n, gx, cut, s_ref, *rest):
    left, right = rest[:n], rest[n : 2 * n]
    full = rest[-1]

    def step(t, carry):
        at = pl.ds(pl.multiple_of(t * 256, 256), 256)
        acc = None
        for a, b in zip(left, right):
            part = lax.dot_general(
                a[:, at], b[...], (((0,), (0,)), ((), ())), preferred_element_type=F32
            )
            acc = part if acc is None else acc + part
        full[at, :] = acc.astype(BF16)
        return carry

    lax.fori_loop(0, full.shape[0] // 256, step, 0)
    size = full.shape[0] // (2 * gx)
    for a, dst in enumerate(rest[2 * n : 2 * n + 2] if cut else ()):
        for k in range(1, gx + 1):
            dst[(k - 1) * size : k * size, :] = full[block_at(s_ref, a, k, gx, size), :]


def block_at(s_ref, a, k, gx, size):
    y = s_ref[2] if a == 0 else 1 - s_ref[2]
    z = lax.rem(s_ref[0] + (2 * gx - k), gx)
    return pl.ds(pl.multiple_of((y * gx + z) * size, 16), size)


def assemble_body(gx, cuts, s_ref, *rest):
    pieces, outs = rest[: 2 * gx], rest[2 * gx :]
    for a in range(2):
        for k in range(gx):
            piece = pieces[a * gx + k]
            start = 0
            for out in outs:
                size = piece.shape[0]
                out[block_at(s_ref, a, k, gx, size), :] = piece[:, start : start + out.shape[1]]
                start += out.shape[1]


def after(value, *others):
    return lax.optimization_barrier((value,) + others)[0]


def layer_norm(values, norm_gain, norm_shift):
    center = values - jnp.mean(values, axis=-1, keepdims=True)
    factor = lax.rsqrt(jnp.mean(center * center, axis=-1, keepdims=True) + EPSILON)
    normal = center * factor
    return (normal * norm_gain + norm_shift, normal, factor)


def norm_back(upstream, normal, factor, norm_gain):
    shaped = upstream * norm_gain
    first_mean = jnp.mean(shaped, axis=-1, keepdims=True)
    second_mean = jnp.mean(shaped * normal, axis=-1, keepdims=True)
    return factor * (shaped - first_mean - normal * second_mean)


def per_device(
    block_input,
    picture,
    position,
    patch_mask,
    gain_attn,
    shift_attn,
    w_query,
    b_query,
    w_key,
    b_key,
    w_value,
    b_value,
    w_out,
    b_out,
    gain_mlp,
    shift_mlp,
    w_up,
    b_up,
    w_down,
    b_down,
    out_grad,
):
    gx = lax.axis_size("gx")
    column = lax.axis_index("gy")
    segment = lax.axis_index("gx")
    micros = block_input.shape[0]
    rows = block_input.shape[2]
    width = block_input.shape[3]
    slots = picture.shape[2]
    qr = 4 * rows
    head_cols = w_query.shape[1]
    hidden_cols = w_up.shape[1]
    heads = head_cols // HEAD_DIM
    dup = gx // heads
    assert lax.axis_size("gy") == 4 and dup * heads == gx and slots == qr * gx
    shard_rows = w_query.shape[0]
    head_start = column * head_cols
    up_start = column * hidden_cols
    where = jnp.stack([segment, column, lax.axis_index("dp")]).astype(jnp.int32)
    x_pairs = [(d, d ^ 2) for d in range(4)]
    core_pairs = [(d, d ^ 1) for d in range(4)]
    spins = [[(d, (d + r) % gx) for d in range(gx)] for r in range(gx)]
    over = ("dp", "gx")

    last_out = [where]

    def chained(kernel, *args):
        out = kernel(after(where, last_out[0]), *args)
        last_out[0] = out[0]
        return out

    def here(*values):
        return lax.optimization_barrier(values + (last_out[0],))[:-1]

    ring = spins[1]
    swap_y = [(0, 1), (1, 0)]
    split = lax.axis_size("dp") == 2 and shard_rows % 16 == 0

    def gather(shard):
        if not split:
            return lax.all_gather(shard, over, axis=0, tiled=True)
        near = [shard]
        for _ in range(1, gx):
            near.append(lax.ppermute(near[-1], "gx", ring))
        return near + [lax.ppermute(piece, "dp", swap_y) for piece in near]

    def ring_step(state, *holds):
        near, far = state
        if split:
            near.append(lax.ppermute(after(near[-1], *holds), "gx", ring))
            far.append(lax.ppermute(near[-1], "dp", swap_y))

    def ring_start(shard, *holds):
        if not split:
            return gather(shard), None
        shard = after(shard, *holds)
        return [shard], [lax.ppermute(shard, "dp", swap_y)]

    def ring_end(state):
        return state[0] + state[1] if split else state[0]

    def assemble(pieces, cuts, name):
        if not split:
            starts = [sum(cuts[:k]) for k in range(len(cuts))]
            return [pieces[:, a : a + c] for a, c in zip(starts, cuts)]
        total = 2 * gx * shard_rows
        kernel = call(
            functools.partial(assemble_body, gx, cuts),
            [SM] + [VM] * (2 * gx),
            [((total, c), BF16) for c in cuts],
            [],
            0,
            4 * total * sum(cuts),
            name,
        )
        return chained(kernel, *pieces)

    def weight_grad(left, right, name, cut=True):
        d1, d2 = left[0].shape[1], right[0].shape[1]
        if not split:
            full = sum(
                lax.dot_general(a, b, (((0,), (0,)), ((), ())), preferred_element_type=F32)
                for a, b in zip(left, right)
            )
            return full.astype(BF16)
        k = sum(a.shape[0] for a in left)
        n = len(left)
        kernel = call(
            functools.partial(weight_grad_body, n, gx, cut),
            [SM] + [VM] * (2 * n),
            [((d1 // 2, d2), BF16)] * 2 if cut else [((d1, d2), BF16)],
            [((d1, d2), BF16)] if cut else [],
            2 * k * d1 * d2,
            2 * (k * (d1 + d2) + d1 * d2),
            name,
        )
        out = chained(kernel, *left, *right)
        return out if cut else out[0]

    def reduce(grads):
        if not split:
            return [
                lax.psum_scatter(g, over, scatter_dimension=0, tiled=True).astype(F32)
                for g in grads
            ]
        pairs = [(keep, lax.ppermute(send, "dp", swap_y)) for keep, send in grads]

        def block(k):
            at = slice(k * shard_rows, (k + 1) * shard_rows)
            return jnp.concatenate([a[at].astype(F32) + b[at].astype(F32) for a, b in pairs], axis=1)

        total = block(0)
        for k in range(1, gx):
            total = block(k) + lax.ppermute(total.astype(BF16), "gx", ring).astype(F32)
        ends = [0]
        for keep, _ in grads:
            ends.append(ends[-1] + keep.shape[1])
        return [total[:, a:b] for a, b in zip(ends[:-1], ends[1:])]

    def pack(q, k, v):
        n = q.shape[0]
        parts = [t.reshape(n, heads, HEAD_DIM) for t in (q, k, v)]
        parts.append(jnp.zeros((n, heads, PACK - 3 * HEAD_DIM), q.dtype))
        return jnp.concatenate(parts, axis=2).reshape(n, heads * PACK)

    def unpack(t):
        n = t.shape[0]
        t = t.reshape(n, heads, PACK)
        return [
            t[:, :, k * HEAD_DIM : (k + 1) * HEAD_DIM].reshape(n, head_cols) for k in range(3)
        ]

    pieces_qkv = gather(pack(w_query, w_key, w_value))
    full_up, full_down = [
        lax.all_gather(w, over, axis=0, tiled=True)
        for w in (w_up, w_down)
    ]
    ring_out = ring_start(w_out, pieces_qkv[-1])
    (full_qkv,) = assemble(pieces_qkv, (heads * PACK,), "join_qkv")
    biases = [
        lax.dynamic_slice_in_dim(b, head_start, head_cols)[None] for b in (b_query, b_key, b_value)
    ]
    qkv_bias = pack(*biases)
    up_bias = lax.dynamic_slice_in_dim(b_up, up_start, hidden_cols)[None]

    def swap(blocks):
        return [blocks[0]] + [lax.ppermute(blocks[r], "gx", spins[r]) for r in range(1, gx)]

    quarter = HEAD_DIM // 4
    inverse = 10000.0 ** (-jnp.arange(quarter, dtype=F32) / quarter)
    places = position[:, :, 0, :].astype(F32)
    angles = jnp.concatenate(
        [inverse[None, :, None] * places[0][:, None], inverse[None, :, None] * places[1][:, None]],
        axis=1,
    )
    cos_all, sin_all = jnp.cos(angles), jnp.sin(angles)
    cos_own = lax.dynamic_slice_in_dim(cos_all, segment * qr, qr, 2)
    sin_own = lax.dynamic_slice_in_dim(sin_all, segment * qr, qr, 2)

    pictures, masks = picture[:, 0], patch_mask[:, 0]
    marks = jnp.where(masks == 1, pictures, 1000 + jnp.arange(slots, dtype=jnp.int32)[None])
    id_row = marks[:, None, :]
    id_col = jnp.broadcast_to(marks[:, :, None], (micros, slots, 128))
    nb = slots // BLK
    own_block = jnp.arange(nb, dtype=jnp.int32)[None]
    first_id, last_id = pictures[:, ::BLK], pictures[:, BLK - 1 :: BLK]
    below = jnp.sum(
        (pictures[:, None, :] < first_id[:, :, None]).astype(jnp.int32), axis=-1
    )
    upto = jnp.sum(
        (pictures[:, None, :] <= last_id[:, :, None]).astype(jnp.int32), axis=-1
    )
    low = jnp.where(masks[:, ::BLK] == 1, below // BLK, own_block)
    top = jnp.where(masks[:, BLK - 1 :: BLK] == 1, (upto - 1) // BLK, own_block)
    limits = jnp.stack([low, top], axis=1)

    tri = 3 * HEAD_DIM
    qkv_call = call(
        functools.partial(qkv_body, gx, dup, rows),
        [SM] + [VM] * 6,
        [((tri, qr), BF16)] * gx + [((qr, width), BF16)],
        [],
        2 * qr * width * gx * PACK,
        2 * (2 * qr * width + width * heads * PACK + gx * tri * qr),
        "qkv",
    )
    work = slots * slots // 2
    attend_call = call(
        functools.partial(attend_body, gx, slots),
        [SM, SM] + [VM] * (gx + 2),
        [((HEAD_DIM, qr), BF16)] * gx
        + [((tri, slots), BF16), ((1, slots), F32)],
        [((HEAD_DIM, slots), BF16), ((slots, HEAD_DIM), BF16)],
        4 * work * PACK,
        2 * 10 * HEAD_DIM * slots,
        "attend",
        work,
    )
    project_call = call(
        functools.partial(project_body, gx, dup, rows),
        [SM] + [VM] * (gx + 1),
        [((qr, head_cols), BF16), ((2 * rows, width), BF16), ((2 * rows, width), BF16)],
        [((head_cols, qr), BF16), ((qr, width), BF16)],
        2 * qr * width * head_cols,
        2 * (2 * qr * head_cols + width * head_cols + qr * width),
        "project",
    )
    half_rows = ((2 * rows, width), BF16)
    mlp_call = call(
        mlp_body,
        [SM] + [VM] * 7,
        [((qr, hidden_cols), BF16)] * 2 + [half_rows] * 4 + [((1, hidden_cols), F32)],
        [],
        8 * qr * width * hidden_cols,
        2 * (4 * qr * width + 2 * width * hidden_cols + 2 * qr * hidden_cols),
        "mlp",
    )
    mix_grad_call = call(
        functools.partial(mix_grad_body, gx, dup, rows),
        [SM] + [VM] * 3,
        [((HEAD_DIM, qr), BF16)] * gx + [((qr, width), BF16)],
        [((head_cols, qr), BF16)],
        2 * qr * width * head_cols,
        2 * (2 * qr * width + width * head_cols + qr * head_cols),
        "mix_grad",
    )
    attend_back_call = call(
        functools.partial(attend_back_body, gx, slots),
        [SM, SM] + [VM] * (6 + gx),
        [((tri, qr), BF16)] * gx,
        [((HEAD_DIM, slots), BF16)]
        + [((slots, HEAD_DIM), BF16)] * 4
        + [((slots, BLK), F32)] * 2
        + [((slots, HEAD_DIM), F32)] * 2
        + [((tri, slots), BF16)],
        10 * work * PACK,
        2 * 10 * HEAD_DIM * slots,
        "attend_back",
        work,
    )
    qkv_back_call = call(
        functools.partial(qkv_back_body, gx, dup, rows),
        [SM] + [VM] * (gx + 1),
        [((qr, heads * PACK), BF16), half_rows, half_rows, ((1, heads * PACK), F32)],
        [((qr, width), BF16)],
        2 * qr * width * heads * PACK,
        2 * (2 * qr * heads * PACK + width * heads * PACK + qr * width),
        "qkv_back",
    )

    inputs = block_input[:, 0].astype(F32)
    normed = layer_norm(inputs, gain_attn, shift_attn)[0].astype(BF16)
    cots = out_grad[:, 0]
    normed_x = lax.ppermute(normed, "gy", x_pairs)
    cots_x = lax.ppermute(after(cots, normed_x), "gy", x_pairs)
    sents, rows_ins = [], []
    for m in range(micros):
        na = jnp.concatenate([normed[m], normed_x[m]], axis=0)
        nb_half = lax.ppermute(na, "gy", core_pairs)
        *sent, rows_in = chained(qkv_call, na, nb_half, full_qkv, qkv_bias, cos_own[m], sin_own[m])
        sents.append(sent)
        rows_ins.append(rows_in)
    heads_in = [None] * micros
    mixeds = [None] * micros
    kept = [None] * micros

    def attend(m):
        *mixed, qkv_full, log_total = chained(
            attend_call, limits[m], *heads_in[m], id_row[m], id_col[m]
        )
        mixeds[m] = mixed
        kept[m] = (qkv_full, log_total)

    def fetch(m):
        sent = sents[m]
        if m:
            sent = here(*sent, heads_in[m - 1][-1])[:-1]
        heads_in[m] = swap(sent)

    def back_mixed(m):
        mixeds[m] = swap(mixeds[m])

    none = lambda: [None] * micros
    mixes, middles, norms, crows, acts, hgs, results, backs = (none() for _ in range(8))
    branch_rows, gots, ds, input_grads, outputs = (none() for _ in range(5))
    sums = dict(gain_mlp=0.0, shift_mlp=0.0, up=0.0, out=0.0, gain_attn=0.0, shift_attn=0.0, qkv=0.0)
    moving = {}

    def core(v):
        return lax.ppermute(v, "gy", core_pairs)

    def cross(v):
        return lax.ppermute(v, "gy", x_pairs)

    def mark(*values):
        last_out[0] = values[0]

    def sum_start(key, m, keep, send):
        moving[key, m] = (keep, core(send))

    def sum_cross(key, m):
        keep, send = here(*moving[key, m])
        both = keep.astype(F32) + send.astype(F32)
        part = both[rows:].astype(BF16)
        mark(part)
        moving[key, m] = (both[:rows], cross(part))

    def sum_end(key, m):
        own, other = here(*moving[key, m])
        return own + other.astype(F32)

    def half(key, m):
        own, other = here(*moving[key, m])
        both = jnp.concatenate([own, other], axis=0)
        mark(both)
        moving[key, m] = (both, core(both))

    def project(m):
        mixes[m], keep, send = chained(project_call, *mixeds[m], full_out)
        sum_start("branch", m, keep, send)

    def norm_two(m):
        middle = inputs[m] + sum_end("branch", m) + b_out
        normed_two, normal_two, factor_two = layer_norm(middle, gain_mlp, shift_mlp)
        middles[m] = middle
        norms[m] = (normal_two, factor_two)
        low_two = normed_two.astype(BF16)
        mark(low_two)
        moving["two", m] = (low_two, cross(low_two))

    def cot_half(m):
        ca = jnp.concatenate([cots[m], cots_x[m]], axis=0)
        crows[m] = (ca, core(ca))

    def mlp(m):
        act, hg, ra, rb, na, nb_half, up_part = chained(
            mlp_call, *moving["two", m], *crows[m], full_up, full_down, up_bias
        )
        acts[m], hgs[m] = act, hg
        sums["up"] += up_part[0]
        sum_start("two_grad", m, na, nb_half)
        results[m] = (ra, rb)

    def norm_two_back(m):
        two_grad = sum_end("two_grad", m)
        normal_two, factor_two = norms[m]
        sums["gain_mlp"] += jnp.sum(two_grad * normal_two, axis=0)
        sums["shift_mlp"] += jnp.sum(two_grad, axis=0)
        middle_grad = cots[m].astype(F32) + norm_back(two_grad, normal_two, factor_two, gain_mlp)
        branch_grad = middle_grad.astype(BF16)
        mark(branch_grad)
        sums["out"] += jnp.sum(branch_grad.astype(F32), axis=0)
        backs[m] = middle_grad
        moving["back", m] = (branch_grad, cross(branch_grad))

    def mix_grad(m):
        *sent, branch_rows[m] = chained(mix_grad_call, *moving["back", m], full_out)
        gots[m] = swap(sent)

    def attend_back(m):
        got = chained(
            attend_back_call,
            limits[m],
            *kept[m],
            id_row[m],
            id_col[m],
            cos_all[m],
            sin_all[m],
            *gots[m],
        )
        gots[m] = swap(got)

    def qkv_back(m):
        ds[m], keep, send, part = chained(qkv_back_call, *gots[m], full_qkv)
        sums["qkv"] += part
        sum_start("one", m, keep, send)

    def norm_one_back(m):
        one_grad = sum_end("one", m)
        _, normal_one, factor_one = layer_norm(inputs[m], gain_attn, shift_attn)
        sums["gain_attn"] += jnp.sum(one_grad * normal_one, axis=0)
        sums["shift_attn"] += jnp.sum(one_grad, axis=0)
        input_grads[m] = backs[m] + norm_back(one_grad, normal_one, factor_one, gain_attn)
        mark(input_grads[m])

    def result_start(m):
        ra, rb = here(*results[m])
        sum_start("result", m, ra, rb)

    def result_end(m):
        outputs[m] = (middles[m] + sum_end("result", m) + b_down).astype(BF16)
        mark(outputs[m])

    halves = [slice(0, 2 * rows), slice(2 * rows, 4 * rows)]
    grads = {}

    def grad_up():
        grads["up"] = weight_grad(
            [t for m in range(micros) for t in moving["two", m]], [t[h] for t in hgs for h in halves], "grad_up", False
        )

    def grad_down():
        grads["down"] = weight_grad(
            [t for c in crows for t in c], [t[h] for t in acts for h in halves], "grad_down", False
        )

    fetch(0)
    for _ in range(1, gx):
        ring_step(ring_out, last_out[0])
    fetch(1)
    attend(0)
    back_mixed(0)
    fetch(2)
    (full_out,) = assemble(ring_end(ring_out), (head_cols,), "join_out")
    attend(1)
    back_mixed(1)
    project(0)
    sum_cross("branch", 0)
    attend(2)
    back_mixed(2)
    norm_two(0)
    project(1)
    sum_cross("branch", 1)
    for m in range(micros):
        cot_half(m)
    half("two", 0)
    project(2)
    sum_cross("branch", 2)
    norm_two(1)
    mlp(0)
    half("two", 1)
    norm_two(2)
    sum_cross("two_grad", 0)
    mlp(1)
    half("two", 2)
    norm_two_back(0)
    sum_cross("two_grad", 1)
    mlp(2)
    half("back", 0)
    norm_two_back(1)
    sum_cross("two_grad", 2)
    mix_grad(0)
    grad_down()
    half("back", 1)
    norm_two_back(2)
    mix_grad(1)
    result_start(0)
    attend_back(0)
    half("back", 2)
    mix_grad(2)
    sum_cross("result", 0)
    result_start(1)
    attend_back(1)
    result_end(0)
    sum_cross("result", 1)
    result_start(2)
    grad_up()
    qkv_back(0)
    sum_cross("result", 2)
    sum_cross("one", 0)
    attend_back(2)
    result_end(1)
    norm_one_back(0)
    qkv_back(1)
    result_end(2)
    sum_cross("one", 1)
    grads["out"] = weight_grad(branch_rows, mixes, "grad_out")
    norm_one_back(1)
    qkv_back(2)
    grads["qkv"] = weight_grad(rows_ins, ds, "grad_qkv")
    sum_cross("one", 2)
    norm_one_back(2)
    grad_up, grad_down = [
        lax.psum_scatter(grads[k], over, scatter_dimension=0, tiled=True).astype(F32)
        for k in ("up", "down")
    ]
    (grad_out,) = reduce([grads["out"]])
    (grad_qkv,) = reduce([grads["qkv"]])
    grad_query, grad_key, grad_value = unpack(grad_qkv)

    def whole(part, start, total):
        return lax.dynamic_update_slice_in_dim(jnp.zeros((total,), F32), part, start, 0)

    vec_q, vec_k, vec_v = [whole(t[0], head_start, b_query.shape[0]) for t in unpack(sums["qkv"])]
    parts = (
        sums["gain_attn"],
        sums["shift_attn"],
        vec_q,
        vec_k,
        vec_v,
        sums["out"],
        sums["gain_mlp"],
        sums["shift_mlp"],
        whole(sums["up"], up_start, b_up.shape[0]),
        jnp.sum(cots.astype(F32), axis=(0, 1)),
    )
    total = jnp.concatenate(parts).reshape(-1, 128)
    for axis in ("gy", "dp", "gx"):
        n = lax.axis_size(axis)
        step = 1
        while step < n:
            total = total + lax.ppermute(total, axis, [(d, d ^ step) for d in range(n)])
            step *= 2
    total = total.reshape(-1)
    vectors = []
    for part in parts:
        vectors.append(total[: part.shape[0]])
        total = total[part.shape[0] :]
    return (
        jnp.stack(outputs)[:, None],
        jnp.stack(input_grads)[:, None],
        vectors[0],
        vectors[1],
        grad_query,
        vectors[2],
        grad_key,
        vectors[3],
        grad_value,
        vectors[4],
        grad_out,
        vectors[5],
        vectors[6],
        vectors[7],
        grad_up,
        vectors[8],
        grad_down,
        vectors[9],
    )


def solution(mesh):
    acts = P(None, "dp", ("gx", "gy"), None)
    ids = P(None, "dp", None)
    weight = P(("dp", "gx"), "gy")
    placed = (acts, ids, P(None, None, "dp", None), ids, P(), P())
    placed += (weight, P()) * 4 + (P(), P()) + (weight, P()) * 2 + (acts,)
    outs = (acts, acts, P(), P()) + (weight, P()) * 4 + (P(), P()) + (weight, P()) * 2
    return jax.shard_map(
        per_device, mesh=mesh, in_specs=placed, out_specs=outs, check_vma=False
    )
```
